32 devices in a mesh: seq: 8 (over y, x, core), head: 4 (over z).
Axes of the slice: x: 2, y: 2, z: 4, core: 2. Of those that a mesh axis runs over, the one named last changes fastest.
Arguments:
- queries: bfloat16 [2, 8, 8, 32, 128], P(None, 'head'), may hold values from -128 to 128
- tree_keys: bfloat16 [2, 8, 32, 128], P(None, 'head'), may hold values from -8 to 8
- tree_values: bfloat16 [2, 8, 32, 128], P(None, 'head'), may hold values from -6 to 6
- cache_keys: bfloat16 [8, 8192, 128], P('head', 'seq'), may hold values from -6 to 6
- cache_values: bfloat16 [8, 8192, 128], P('head', 'seq'), may hold values from -6 to 6
- block_ids: int32 [8, 32], P('head'), may hold values from 0 to 63, as said below
- ancestors: int32 [1, 32, 32], replicated, may hold values from 0 to 1, as said below
- out_weight: bfloat16 [8192, 8192], P('seq', 'head'), may hold values from -0.0625 to 0.0625
Outputs:
- draft_mixed: bfloat16 [32, 1, 8192], P('seq', None, 'head')
- verify_mixed: bfloat16 [32, 1, 8192], P('seq', None, 'head')
The draws below stay inside these ranges and needn't reach their ends.
Inputs may be any that keep to these rules, and one draw needn't show every extreme that they name: `block_ids`: the 32 block numbers of one pair are distinct, and for every pair one run of 1024 positions (positions s * 1024 to (s + 1) * 1024 - 1 for some s) holds at least half of its 32 blocks, or all 8 blocks of the run where the run has fewer. ancestors[r, n, k] is 1 exactly when k is n or an ancestor of n in request r's tree; node 0 is the root and every other node's parent has a smaller number.
All inputs are finite; a program needn't handle non-finite values.
Results may differ from the reference program's by a relative error of at most 0.009.
Values may be sent and summed in bfloat16 or wider, within the bound.
A program may use at most 64 MiB of HBM per device.

```python
import jax
import jax.numpy as jnp
from jax import lax

D = 8192
HQ = 64
KVH = 8
HD = 128
G = 8
NODES = 32
SEL = 32
BLOCK = 128
PAIRS = 8
REQUESTS = 1
CONTEXT = 8192
BLOCKS_DEV = 8
BLOCKS = 64
N_SEQ = 8


def tree_draw(base_key):
    own_keys = jnp.clip(jax.random.normal(jax.random.fold_in(base_key, 101), (2, PAIRS, NODES, HD), jnp.float32), -6.0, 6.0)
    jitter = jnp.clip(jax.random.normal(jax.random.fold_in(base_key, 102), (2, PAIRS, G, NODES, HD), jnp.float32), -6.0, 6.0)
    query_rows = 3.0 * jitter + 1.1 * own_keys[:, :, None]
    return (jnp.clip(query_rows, -128.0, 128.0), own_keys)


def draw_queries(key, part):
    return tree_draw(key)[0].astype(jnp.bfloat16)


def draw_tree_keys(key, part):
    return tree_draw(key)[1].astype(jnp.bfloat16)


def draw_block_ids(key, part):
    key_one = jax.random.fold_in(key, 201)
    key_two = jax.random.fold_in(key, 202)
    key_three = jax.random.fold_in(key, 203)
    hot_shard = jax.random.randint(key_one, (PAIRS, 1), 0, N_SEQ)
    ranked = jax.random.randint(key_two, (PAIRS, BLOCKS), 0, 1 << 19) * BLOCKS + jnp.arange(BLOCKS, dtype=jnp.int32)[None, :]
    local_rank = jax.vmap(lambda one_key: jax.random.permutation(one_key, BLOCKS_DEV))(jax.random.split(key_three, PAIRS)).astype(jnp.int32)
    block_numbers = jnp.arange(BLOCKS, dtype=jnp.int32)
    owner_shard = (block_numbers // BLOCKS_DEV)[None, :]
    rank_of_block = jnp.take(local_rank, block_numbers % BLOCKS_DEV, axis=1)
    preferred = jnp.logical_and(owner_shard == hot_shard, rank_of_block < min(SEL // 2, BLOCKS_DEV))
    ranked = jnp.where(preferred, ranked - (1 << 30), ranked)
    return jnp.argsort(ranked, axis=1, stable=True)[:, :SEL].astype(jnp.int32)


def draw_ancestors(key, part):

    def per_request(request_key):
        limits = jnp.maximum(jnp.arange(NODES, dtype=jnp.int32), 1)
        parents = jax.random.randint(request_key, (NODES,), 0, limits)
        identity_rows = jnp.eye(NODES, dtype=jnp.int32)

        def extend(position, lineage):
            return lineage.at[position].set(jnp.maximum(lineage[parents[position]], identity_rows[position]))
        return lax.fori_loop(1, NODES, extend, identity_rows)
    return jax.vmap(per_request)(jax.random.split(key, REQUESTS))


def level_of(own_key, shape, cuts, low, largest):
    def one(dim, blocks):
        steps = jax.random.uniform(jax.random.fold_in(jax.random.fold_in(own_key, 6), dim), (blocks,), jnp.float32, low / len(cuts), largest / len(cuts))
        return jnp.repeat(jnp.exp(steps), shape[dim] // blocks).reshape((-1,) + (1,) * (len(shape) - dim - 1))

    factor_of = one(*cuts[0])
    for cut in cuts[1:]:
        factor_of = factor_of * one(*cut)
    return factor_of


def normal_values(own_key, extent, width, reach, cuts=(), kind=jnp.bfloat16):
    values = jax.random.normal(own_key, extent, jnp.float32) * width
    if len(cuts) > 0:
        values = level_of(own_key, extent, cuts, -0.22, 0.18) * values
    return jnp.clip(values, min=-reach, max=reach).astype(kind)


def setup_inputs(seed: int = 0) -> dict:
    seeds = jax.random.split(jax.random.key(seed), 9)
    return {
        "queries": draw_queries(jax.random.fold_in(seeds[8], 71), 0),
        "tree_keys": draw_tree_keys(jax.random.fold_in(seeds[8], 71), 0),
        "tree_values": normal_values(seeds[2], (2, PAIRS, NODES, HD), 1.0, 6.0, ((1, 4),)),
        "cache_keys": normal_values(seeds[3], (PAIRS, CONTEXT, HD), 1.0, 6.0, ((0, 4), (1, 8))),
        "cache_values": normal_values(seeds[4], (PAIRS, CONTEXT, HD), 1.0, 6.0, ((0, 4), (1, 8))),
        "block_ids": draw_block_ids(jax.random.fold_in(seeds[8], 71), 0),
        "ancestors": draw_ancestors(jax.random.fold_in(seeds[8], 71), 0),
        "out_weight": normal_values(seeds[7], (HQ * HD, D), (HQ * HD) ** -0.5, 0.0625, ((0, 8), (1, 4))),
    }


def attend(query_rows, key_rows, value_rows, tree_key_rows, tree_value_rows, tree_mask):
    score_scale = HD ** -0.5
    cache_scores = jnp.einsum("gnh,lh->gnl", query_rows.astype(jnp.float32), key_rows.astype(jnp.float32)) * score_scale
    tree_scores = jnp.einsum("gnh,kh->gnk", query_rows.astype(jnp.float32), tree_key_rows.astype(jnp.float32)) * score_scale
    allowed = tree_mask[None] > 0
    tree_scores = jnp.where(allowed, tree_scores, -1e30)
    peak = jnp.maximum(jnp.max(cache_scores, axis=-1), jnp.max(tree_scores, axis=-1))[..., None]
    cache_weights = jnp.exp(cache_scores - peak)
    tree_weights = jnp.where(allowed, jnp.exp(tree_scores - peak), 0.0)
    totals = jnp.sum(cache_weights, axis=-1) + jnp.sum(tree_weights, axis=-1)
    summed = jnp.einsum("gnl,lh->gnh", cache_weights.astype(jnp.bfloat16).astype(jnp.float32), value_rows.astype(jnp.float32))
    summed = summed + jnp.einsum("gnk,kh->gnh", tree_weights.astype(jnp.bfloat16).astype(jnp.float32), tree_value_rows.astype(jnp.float32))
    result = summed / totals[..., None]
    return jnp.transpose(result, (1, 0, 2)).astype(jnp.bfloat16)


def reference(queries, tree_keys, tree_values, cache_keys, cache_values, block_ids, ancestors, out_weight):
    def per_pair(pair_index):
        key_rows = cache_keys[pair_index]
        value_rows = cache_values[pair_index]
        chosen_ids = block_ids[pair_index]
        tree_mask = ancestors[pair_index // KVH]
        picked_keys = key_rows.reshape(BLOCKS, BLOCK, HD)[chosen_ids].reshape(SEL * BLOCK, HD)
        picked_values = value_rows.reshape(BLOCKS, BLOCK, HD)[chosen_ids].reshape(SEL * BLOCK, HD)
        draft_rows = attend(queries[0, pair_index], picked_keys, picked_values, tree_keys[0, pair_index], tree_values[0, pair_index], tree_mask)
        verify_rows = attend(queries[1, pair_index], key_rows, value_rows, tree_keys[1, pair_index], tree_values[1, pair_index], tree_mask)
        return draft_rows, verify_rows

    drafts, verifies = lax.map(per_pair, jnp.arange(PAIRS, dtype=jnp.int32))

    def project_out(attended):
        flat_rows = attended.reshape(REQUESTS, KVH, NODES, G * HD)
        flat_rows = jnp.transpose(flat_rows, (2, 0, 1, 3)).reshape(NODES * REQUESTS, HQ * HD)
        mixed = jnp.dot(flat_rows, out_weight, preferred_element_type=jnp.float32)
        return mixed.astype(jnp.bfloat16).reshape(NODES, REQUESTS, D)

    return project_out(drafts), project_out(verifies)
```

```python
import functools
import math

import jax
import jax.numpy as jnp
import numpy as np
from jax import lax
from jax.experimental import pallas as pl
from jax.experimental.pallas import tpu as pltpu
from jax.sharding import PartitionSpec as P

KVH = 8
BLOCK = 128
MESH = pl.DeviceIdType.MESH
F32 = jnp.float32
BF16 = jnp.bfloat16


def flip(index, mask):
    out = index
    bit = 1
    while bit <= mask:
        if mask & bit:
            out = out + bit * (1 - 2 * ((index // bit) % 2))
        bit *= 2
    return out


def contract(left, right, left_dim, right_dim):
    return lax.dot_general(
        left, right, (((left_dim,), (right_dim,)), ((), ())), preferred_element_type=F32
    )


def kernel(
    dims,
    ids_ref,
    anc_ref,
    spread_ref,
    order_ref,
    tk_ref,
    tv_ref,
    q_hbm,
    k_hbm,
    v_hbm,
    w_hbm,
    draft_ref,
    verify_ref,
    q_v,
    k_v,
    v_v,
    w_v,
    acc_out,
    stat_out,
    acc_in,
    stat_in,
    zbuf,
    parts,
    mix_out,
    mix_in,
    load_sem,
    s1,
    r1,
    s1s,
    r1s,
    s2,
    r2,
    s3,
    r3,
    s4,
    r4,
):
    seq_n, head_n, pair_dev, groups, nodes, requests, hd, heads_dev = dims
    me = lax.axis_index("seq")
    z = lax.axis_index("head")
    blocks = 2 * pair_dev
    per_block = seq_n // blocks
    rows = groups * nodes
    chunk = rows // per_block
    chunk_heads = chunk // nodes
    pieces = heads_dev // chunk_heads
    ctx = k_v.shape[1]
    blocks_dev = ctx // BLOCK
    node_dev = nodes // seq_n
    out_rows = 2 * node_dev * requests
    factor2 = hd ** (-0.5) * math.log2(math.e)

    loads = []
    for i, (src, dst) in enumerate(((k_hbm, k_v), (q_hbm, q_v), (v_hbm, v_v), (w_hbm, w_v))):
        copy = pltpu.make_async_copy(src, dst, load_sem.at[i])
        copy.start()
        loads.append(copy)

    barrier = pltpu.get_barrier_semaphore()
    for k in range(1, seq_n):
        pl.semaphore_signal(barrier, inc=1, device_id={"seq": flip(me, k)}, device_id_type=MESH)
    for k in range(1, head_n):
        pl.semaphore_signal(barrier, inc=1, device_id={"head": flip(z, k)}, device_id_type=MESH)

    loads[0].wait()
    loads[1].wait()
    own_block = me // per_block
    own_piece = me % per_block
    owned = me * blocks_dev + lax.broadcasted_iota(jnp.int32, (blocks_dev, 1), 0)

    sends = []
    for step in reversed(range(blocks)):
        block = flip(own_block, step)
        attention = block // pair_dev
        pair = block % pair_dev
        hit = (ids_ref[pair] == owned).astype(F32)
        chosen = jnp.max(hit, axis=1, keepdims=True)
        chosen = jnp.maximum(chosen, attention.astype(F32))
        bias = (chosen - 1.0) * 1e30
        scores = contract(k_v[pair], q_v[block], 1, 1)
        masked = [
            scores[b * BLOCK : (b + 1) * BLOCK] + bias[b : b + 1, :] for b in range(blocks_dev)
        ]
        top = functools.reduce(jnp.maximum, masked)
        peak = jnp.max(top, axis=0, keepdims=True)
        weights = [jnp.exp2((part - peak) * factor2) for part in masked]
        total = jnp.sum(functools.reduce(jnp.add, weights), axis=0, keepdims=True)
        rounded = jnp.concatenate([part.astype(BF16) for part in weights], axis=0)
        if step == blocks - 1:
            loads[2].wait()
        summed = contract(v_v[pair], rounded, 0, 0)
        for piece in range(per_block):
            columns = slice(piece * chunk, (piece + 1) * chunk)
            acc_out[step, piece] = summed[:, columns].astype(BF16)
            stat_out[step, piece, 0:1, :] = peak[:, columns]
            stat_out[step, piece, 1:2, :] = total[:, columns]
        if step == blocks - 1:
            pl.semaphore_wait(barrier, seq_n + head_n - 2)
        for j in range(per_block):
            k = step * per_block + j
            if k == 0:
                continue
            piece = flip(own_piece, j)
            target = flip(me, k)
            for src, dst, ss, rs in (
                (acc_out, acc_in, s1, r1),
                (stat_out, stat_in, s1s, r1s),
            ):
                copy = pltpu.make_async_remote_copy(
                    src_ref=src.at[step, piece],
                    dst_ref=dst.at[k],
                    send_sem=ss.at[k],
                    recv_sem=rs.at[k],
                    device_id={"seq": target},
                    device_id_type=MESH,
                )
                copy.start()
                sends.append(copy)
    first = list(sends)

    own_attention = own_block // pair_dev
    own_pair = own_block % pair_dev
    request = (z * pair_dev + own_pair) // KVH
    own_rows = q_v[own_block, pl.ds(pl.multiple_of(own_piece * chunk, chunk), chunk), :]
    tree_scores = contract(tk_ref[own_block], own_rows, 1, 1)
    allowed = contract(anc_ref[request].astype(F32).astype(BF16), spread_ref[...], 0, 0)
    tree_scores = jnp.where(allowed > 0.5, tree_scores, -1e30)
    tree_peak = jnp.max(tree_scores, axis=0, keepdims=True)
    tree_weights = jnp.exp2((tree_scores - tree_peak) * factor2)
    tree_total = jnp.sum(tree_weights, axis=0, keepdims=True)
    tree_sum = contract(tv_ref[own_block], tree_weights.astype(BF16), 0, 0)

    for copy in first:
        copy.wait_recv()
    peaks = [tree_peak, stat_out[0, own_piece, 0:1, :]]
    totals = [tree_total, stat_out[0, own_piece, 1:2, :]]
    for k in range(1, seq_n):
        peaks.append(stat_in[k, 0:1, :])
        totals.append(stat_in[k, 1:2, :])
    highest = functools.reduce(jnp.maximum, peaks)
    factors = [jnp.exp2((peak - highest) * factor2) for peak in peaks]
    total = functools.reduce(jnp.add, [t * f for t, f in zip(totals, factors)])
    summed = tree_sum * factors[0] + acc_out[0, own_piece].astype(F32) * factors[1]
    for k in range(1, seq_n):
        summed = summed + acc_in[k].astype(F32) * factors[k + 1]
    zbuf[0] = jnp.transpose(summed / total).astype(BF16)

    hops = []
    for k in range(1, head_n):
        copy = pltpu.make_async_remote_copy(
            src_ref=zbuf.at[0],
            dst_ref=zbuf.at[k],
            send_sem=s2.at[k],
            recv_sem=r2.at[k],
            device_id={"head": flip(z, k)},
            device_id_type=MESH,
        )
        copy.start()
        hops.append(copy)
    routes = []
    for k in range(head_n):
        if k > 0:
            hops[k - 1].wait_recv()
        origin = flip(z, k)
        whole_pair = origin * pair_dev + own_pair
        first_head = (whole_pair % KVH) * groups + own_piece * chunk_heads
        target = first_head // heads_dev
        slot = (own_attention * requests + whole_pair // KVH) * pieces + (
            first_head % heads_dev
        ) // chunk_heads

        remote = pltpu.make_async_remote_copy(
            src_ref=zbuf.at[k],
            dst_ref=parts.at[slot],
            send_sem=s3.at[k],
            recv_sem=r3.at[slot],
            device_id={"seq": target},
            device_id_type=MESH,
        )
        here = pltpu.make_async_copy(zbuf.at[k], parts.at[slot], r3.at[slot])

        @pl.when(target != me)
        def _():
            remote.start()

        @pl.when(target == me)
        def _():
            here.start()

        routes.append((target, remote))

    loads[3].wait()
    for slot in range(2 * requests * pieces):
        pltpu.make_async_copy(zbuf.at[0], parts.at[slot], r3.at[slot]).wait()
    stacked = jnp.concatenate(
        [
            jnp.concatenate(
                [
                    parts[lead * pieces + piece, h * nodes : (h + 1) * nodes, :]
                    for piece in range(pieces)
                    for h in range(chunk_heads)
                ],
                axis=1,
            )
            for lead in range(2 * requests)
        ],
        axis=0,
    )
    ordered = contract(order_ref[...], stacked, 1, 0).astype(BF16)
    columns = w_v.shape[1]
    halves = mix_out.shape[0]
    width = columns // halves
    last = []
    for half in range(halves):
        mixed = contract(ordered, w_v[:, half * width : (half + 1) * width], 1, 0)
        for t in range(seq_n):
            mix_out[half, t] = mixed[t * out_rows : (t + 1) * out_rows].astype(BF16)
        for k in reversed(range(1, seq_n)):
            target = flip(me, k)
            copy = pltpu.make_async_remote_copy(
                src_ref=mix_out.at[half, target],
                dst_ref=mix_in.at[half, k],
                send_sem=s4.at[half, k],
                recv_sem=r4.at[half, k],
                device_id={"seq": target},
                device_id_type=MESH,
            )
            copy.start()
            last.append((half, copy))
    for half in range(halves):
        for h, copy in last:
            if h == half:
                copy.wait_recv()
        result = mix_out[half, me].astype(F32)
        for k in range(1, seq_n):
            result = result + mix_in[half, k].astype(F32)
        span = slice(half * width, (half + 1) * width)
        draft_ref[:, span] = result[: out_rows // 2].astype(BF16)
        verify_ref[:, span] = result[out_rows // 2 :].astype(BF16)

    for copy in first:
        copy.wait_send()
    for copy in hops:
        copy.wait_send()
    for target, remote in routes:

        @pl.when(target != me)
        def _():
            remote.wait_send()

    for _, copy in last:
        copy.wait_send()


def local(
    queries, tree_keys, tree_values, cache_keys, cache_values, block_ids, ancestors, out_weight
):
    _, pair_dev, groups, nodes, hd = queries.shape
    ctx = cache_keys.shape[1]
    requests = ancestors.shape[0]
    rows_dev, columns = out_weight.shape
    seq_n = lax.axis_size("seq")
    head_n = lax.axis_size("head")
    heads_dev = rows_dev // hd
    blocks = 2 * pair_dev
    per_block = seq_n // blocks
    rows = groups * nodes
    chunk = rows // per_block
    node_dev = nodes // seq_n
    halves = 2
    width = columns // halves
    out_rows = 2 * node_dev * requests
    all_rows = 2 * requests * nodes
    slots = 2 * requests * heads_dev * nodes // chunk

    spread = (np.arange(chunk)[None, :] % nodes == np.arange(nodes)[:, None]).astype(np.float32)
    order = np.zeros((all_rows, all_rows), np.float32)
    for a in range(2):
        for r in range(requests):
            for n in range(nodes):
                t, j = divmod(n, node_dev)
                row = t * out_rows + a * (node_dev * requests) + j * requests + r
                order[row, (a * requests + r) * nodes + n] = 1.0

    dims = (seq_n, head_n, pair_dev, groups, nodes, requests, hd, heads_dev)
    vmem = pl.BlockSpec(memory_space=pltpu.VMEM)
    anywhere = pl.BlockSpec(memory_space=pl.ANY)
    shape = jax.ShapeDtypeStruct((node_dev * requests, columns), BF16)
    dma = pltpu.SemaphoreType.DMA
    draft, verify = pl.pallas_call(
        functools.partial(kernel, dims),
        out_shape=(shape, shape),
        in_specs=[vmem] * 6 + [anywhere] * 4,
        out_specs=(vmem, vmem),
        scratch_shapes=[
            pltpu.VMEM((blocks, rows, hd), BF16),
            pltpu.VMEM((pair_dev, ctx, hd), BF16),
            pltpu.VMEM((pair_dev, ctx, hd), BF16),
            pltpu.VMEM((rows_dev, columns), BF16),
            pltpu.VMEM((blocks, per_block, hd, chunk), BF16),
            pltpu.VMEM((blocks, per_block, 8, chunk), F32),
            pltpu.VMEM((seq_n, hd, chunk), BF16),
            pltpu.VMEM((seq_n, 8, chunk), F32),
            pltpu.VMEM((head_n, chunk, hd), BF16),
            pltpu.VMEM((slots, chunk, hd), BF16),
            pltpu.VMEM((halves, seq_n, out_rows, width), BF16),
            pltpu.VMEM((halves, seq_n, out_rows, width), BF16),
            dma((4,)),
            dma((seq_n,)),
            dma((seq_n,)),
            dma((seq_n,)),
            dma((seq_n,)),
            dma((head_n,)),
            dma((head_n,)),
            dma((head_n,)),
            dma((slots,)),
            dma((halves, seq_n)),
            dma((halves, seq_n)),
        ],
        compiler_params=pltpu.CompilerParams(
            collective_id=0, has_side_effects=True, vmem_limit_bytes=40 * 1024 * 1024
        ),
        name="tree_attention",
    )(
        block_ids.reshape(pair_dev, 1, block_ids.shape[1]),
        ancestors,
        jnp.asarray(spread, BF16),
        jnp.asarray(order, BF16),
        tree_keys.reshape(blocks, nodes, hd),
        tree_values.reshape(blocks, nodes, hd),
        queries.reshape(blocks, rows, hd),
        cache_keys,
        cache_values,
        out_weight,
    )
    final = (node_dev, requests, columns)
    return draft.reshape(final), verify.reshape(final)


def solution(mesh):
    in_specs = (
        P(None, "head", None, None, None),
        P(None, "head", None, None),
        P(None, "head", None, None),
        P("head", "seq", None),
        P("head", "seq", None),
        P("head", None),
        P(),
        P("seq", "head"),
    )
    out_specs = (P("seq", None, "head"), P("seq", None, "head"))
    return jax.shard_map(local, mesh=mesh, in_specs=in_specs, out_specs=out_specs, check_vma=False)
```

```python
import functools
import math

import jax
import jax.numpy as jnp
import numpy as np
from jax import lax
from jax.experimental import pallas as pl
from jax.experimental.pallas import tpu as pltpu
from jax.sharding import PartitionSpec as P

KVH = 8
BLOCK = 128
MESH = pl.DeviceIdType.MESH
F32 = jnp.float32
BF16 = jnp.bfloat16


def flip(index, mask):
    out = index
    bit = 1
    while bit <= mask:
        if mask & bit:
            out = out + bit * (1 - 2 * ((index // bit) % 2))
        bit *= 2
    return out


def contract(left, right, left_dim, right_dim):
    return lax.dot_general(
        left, right, (((left_dim,), (right_dim,)), ((), ())), preferred_element_type=F32
    )


def kernel(
    dims,
    ids_hbm,
    anc_hbm,
    spread_hbm,
    order_hbm,
    tk_hbm,
    tv_hbm,
    q_hbm,
    k_hbm,
    v_hbm,
    w_hbm,
    out_ref,
    ids_ref,
    anc_ref,
    spread_ref,
    order_ref,
    tk_ref,
    tv_ref,
    q_v,
    k_v,
    v_v,
    w_v,
    acc_out,
    stat_out,
    acc_in,
    stat_in,
    zbuf,
    parts,
    mix_out,
    mix_in,
    load_sem,
    s1,
    r1,
    s1s,
    r1s,
    s2,
    r2,
    s3,
    r3,
    s4,
    r4,
):
    seq_n, head_n, pair_dev, groups, nodes, requests, hd, heads_dev = dims
    me = lax.axis_index("seq")
    z = lax.axis_index("head")
    blocks = 2 * pair_dev
    per_block = seq_n // blocks
    rows = groups * nodes
    chunk = rows // per_block
    chunk_heads = chunk // nodes
    pieces = heads_dev // chunk_heads
    ctx = k_v.shape[1]
    blocks_dev = ctx // BLOCK
    node_dev = nodes // seq_n
    out_rows = 2 * node_dev * requests
    factor2 = hd ** (-0.5) * math.log2(math.e)

    loads = []
    sources = (ids_hbm, q_hbm, k_hbm, v_hbm, tk_hbm, tv_hbm, anc_hbm, spread_hbm, order_hbm, w_hbm)
    places = (ids_ref, q_v, k_v, v_v, tk_ref, tv_ref, anc_ref, spread_ref, order_ref, w_v)
    for i, (src, dst) in enumerate(zip(sources, places)):
        copy = pltpu.make_async_copy(src, dst, load_sem.at[i])
        copy.start()
        loads.append(copy)

    barrier = pltpu.get_barrier_semaphore()
    for k in range(1, seq_n):
        pl.semaphore_signal(barrier, inc=1, device_id={"seq": flip(me, k)}, device_id_type=MESH)
    for k in range(1, head_n):
        pl.semaphore_signal(barrier, inc=1, device_id={"head": flip(z, k)}, device_id_type=MESH)

    for copy in loads[:3]:
        copy.wait()
    own_block = me // per_block
    own_piece = me % per_block
    owned = me * blocks_dev + lax.broadcasted_iota(jnp.int32, (blocks_dev, 1), 0)

    sends = []
    for step in reversed(range(blocks)):
        block = flip(own_block, step)
        attention = block // pair_dev
        pair = block % pair_dev
        hit = (ids_ref[pair] == owned).astype(F32)
        chosen = jnp.max(hit, axis=1, keepdims=True)
        chosen = jnp.maximum(chosen, attention.astype(F32))
        bias = (chosen - 1.0) * 1e30
        scores = contract(k_v[pair], q_v[block], 1, 1)
        masked = [
            scores[b * BLOCK : (b + 1) * BLOCK] + bias[b : b + 1, :] for b in range(blocks_dev)
        ]
        top = functools.reduce(jnp.maximum, masked)
        peak = jnp.max(top, axis=0, keepdims=True)
        weights = [jnp.exp2((part - peak) * factor2) for part in masked]
        total = jnp.sum(functools.reduce(jnp.add, weights), axis=0, keepdims=True)
        rounded = jnp.concatenate([part.astype(BF16) for part in weights], axis=0)
        if step == blocks - 1:
            loads[3].wait()
        summed = contract(v_v[pair], rounded, 0, 0)
        for piece in range(per_block):
            columns = slice(piece * chunk, (piece + 1) * chunk)
            acc_out[step, piece] = summed[:, columns].astype(BF16)
            stat_out[step, piece, 0:1, :] = peak[:, columns]
            stat_out[step, piece, 1:2, :] = total[:, columns]
        if step == blocks - 1:
            pl.semaphore_wait(barrier, seq_n + head_n - 2)
        for j in range(per_block):
            k = step * per_block + j
            if k == 0:
                continue
            piece = flip(own_piece, j)
            target = flip(me, k)
            for src, dst, ss, rs in (
                (acc_out, acc_in, s1, r1),
                (stat_out, stat_in, s1s, r1s),
            ):
                copy = pltpu.make_async_remote_copy(
                    src_ref=src.at[step, piece],
                    dst_ref=dst.at[k],
                    send_sem=ss.at[k],
                    recv_sem=rs.at[k],
                    device_id={"seq": target},
                    device_id_type=MESH,
                )
                copy.start()
                sends.append(copy)
    first = list(sends)

    for copy in loads[4:8]:
        copy.wait()
    own_attention = own_block // pair_dev
    own_pair = own_block % pair_dev
    request = (z * pair_dev + own_pair) // KVH
    own_rows = q_v[own_block, pl.ds(pl.multiple_of(own_piece * chunk, chunk), chunk), :]
    tree_scores = contract(tk_ref[own_block], own_rows, 1, 1)
    allowed = contract(anc_ref[request].astype(F32).astype(BF16), spread_ref[...], 0, 0)
    tree_scores = jnp.where(allowed > 0.5, tree_scores, -1e30)
    tree_peak = jnp.max(tree_scores, axis=0, keepdims=True)
    tree_weights = jnp.exp2((tree_scores - tree_peak) * factor2)
    tree_total = jnp.sum(tree_weights, axis=0, keepdims=True)
    tree_sum = contract(tv_ref[own_block], tree_weights.astype(BF16), 0, 0)

    for copy in first:
        copy.wait_recv()
    peaks = [tree_peak, stat_out[0, own_piece, 0:1, :]]
    totals = [tree_total, stat_out[0, own_piece, 1:2, :]]
    for k in range(1, seq_n):
        peaks.append(stat_in[k, 0:1, :])
        totals.append(stat_in[k, 1:2, :])
    highest = functools.reduce(jnp.maximum, peaks)
    factors = [jnp.exp2((peak - highest) * factor2) for peak in peaks]
    total = functools.reduce(jnp.add, [t * f for t, f in zip(totals, factors)])
    summed = tree_sum * factors[0] + acc_out[0, own_piece].astype(F32) * factors[1]
    for k in range(1, seq_n):
        summed = summed + acc_in[k].astype(F32) * factors[k + 1]
    zbuf[0] = jnp.transpose(summed / total).astype(BF16)

    hops = []
    for k in range(1, head_n):
        copy = pltpu.make_async_remote_copy(
            src_ref=zbuf.at[0],
            dst_ref=zbuf.at[k],
            send_sem=s2.at[k],
            recv_sem=r2.at[k],
            device_id={"head": flip(z, k)},
            device_id_type=MESH,
        )
        copy.start()
        hops.append(copy)
    routes = []
    for k in range(head_n):
        if k > 0:
            hops[k - 1].wait_recv()
        origin = flip(z, k)
        whole_pair = origin * pair_dev + own_pair
        first_head = (whole_pair % KVH) * groups + own_piece * chunk_heads
        target = first_head // heads_dev
        slot = (own_attention * requests + whole_pair // KVH) * pieces + (
            first_head % heads_dev
        ) // chunk_heads

        remote = pltpu.make_async_remote_copy(
            src_ref=zbuf.at[k],
            dst_ref=parts.at[slot],
            send_sem=s3.at[k],
            recv_sem=r3.at[slot],
            device_id={"seq": target},
            device_id_type=MESH,
        )
        here = pltpu.make_async_copy(zbuf.at[k], parts.at[slot], r3.at[slot])

        @pl.when(target != me)
        def _():
            remote.start()

        @pl.when(target == me)
        def _():
            here.start()

        routes.append((target, remote))

    for copy in loads[8:]:
        copy.wait()
    for slot in range(2 * requests * pieces):
        pltpu.make_async_copy(zbuf.at[0], parts.at[slot], r3.at[slot]).wait()
    stacked = jnp.concatenate(
        [
            jnp.concatenate(
                [
                    parts[lead * pieces + piece, h * nodes : (h + 1) * nodes, :]
                    for piece in range(pieces)
                    for h in range(chunk_heads)
                ],
                axis=1,
            )
            for lead in range(2 * requests)
        ],
        axis=0,
    )
    ordered = contract(order_ref[...], stacked, 1, 0).astype(BF16)
    columns = w_v.shape[1]
    halves = mix_out.shape[0]
    width = columns // halves
    last = []
    for half in range(halves):
        mixed = contract(ordered, w_v[:, half * width : (half + 1) * width], 1, 0)
        for t in range(seq_n):
            mix_out[half, t] = mixed[t * out_rows : (t + 1) * out_rows].astype(BF16)
        for k in reversed(range(1, seq_n)):
            target = flip(me, k)
            copy = pltpu.make_async_remote_copy(
                src_ref=mix_out.at[half, target],
                dst_ref=mix_in.at[half, k],
                send_sem=s4.at[half, k],
                recv_sem=r4.at[half, k],
                device_id={"seq": target},
                device_id_type=MESH,
            )
            copy.start()
            last.append((half, copy))
    for half in range(halves):
        for h, copy in last:
            if h == half:
                copy.wait_recv()
        result = mix_out[half, me].astype(F32)
        for k in range(1, seq_n):
            result = result + mix_in[half, k].astype(F32)
        span = slice(half * width, (half + 1) * width)
        out_ref[:, span] = result.astype(BF16)

    for copy in first:
        copy.wait_send()
    for copy in hops:
        copy.wait_send()
    for target, remote in routes:

        @pl.when(target != me)
        def _():
            remote.wait_send()

    for _, copy in last:
        copy.wait_send()


def local(
    queries, tree_keys, tree_values, cache_keys, cache_values, block_ids, ancestors, out_weight
):
    _, pair_dev, groups, nodes, hd = queries.shape
    ctx = cache_keys.shape[1]
    requests = ancestors.shape[0]
    rows_dev, columns = out_weight.shape
    seq_n = lax.axis_size("seq")
    head_n = lax.axis_size("head")
    heads_dev = rows_dev // hd
    blocks = 2 * pair_dev
    per_block = seq_n // blocks
    rows = groups * nodes
    chunk = rows // per_block
    node_dev = nodes // seq_n
    halves = 2
    width = columns // halves
    out_rows = 2 * node_dev * requests
    all_rows = 2 * requests * nodes
    slots = 2 * requests * heads_dev * nodes // chunk

    spread = (np.arange(chunk)[None, :] % nodes == np.arange(nodes)[:, None]).astype(np.float32)
    order = np.zeros((all_rows, all_rows), np.float32)
    for a in range(2):
        for r in range(requests):
            for n in range(nodes):
                t, j = divmod(n, node_dev)
                row = t * out_rows + a * (node_dev * requests) + j * requests + r
                order[row, (a * requests + r) * nodes + n] = 1.0

    dims = (seq_n, head_n, pair_dev, groups, nodes, requests, hd, heads_dev)
    vmem = pl.BlockSpec(memory_space=pltpu.VMEM)
    hbm = pl.BlockSpec(memory_space=pltpu.HBM)
    shape = jax.ShapeDtypeStruct((out_rows, columns), BF16)
    dma = pltpu.SemaphoreType.DMA
    mixed = pl.pallas_call(
        functools.partial(kernel, dims),
        out_shape=shape,
        in_specs=[hbm] * 10,
        out_specs=vmem,
        scratch_shapes=[
            pltpu.VMEM((pair_dev, 1, block_ids.shape[1]), jnp.int32),
            pltpu.VMEM((requests, nodes, nodes), jnp.int32),
            pltpu.VMEM(spread.shape, BF16),
            pltpu.VMEM(order.shape, BF16),
            pltpu.VMEM((blocks, nodes, hd), BF16),
            pltpu.VMEM((blocks, nodes, hd), BF16),
            pltpu.VMEM((blocks, rows, hd), BF16),
            pltpu.VMEM((pair_dev, ctx, hd), BF16),
            pltpu.VMEM((pair_dev, ctx, hd), BF16),
            pltpu.VMEM((rows_dev, columns), BF16),
            pltpu.VMEM((blocks, per_block, hd, chunk), BF16),
            pltpu.VMEM((blocks, per_block, 8, chunk), F32),
            pltpu.VMEM((seq_n, hd, chunk), BF16),
            pltpu.VMEM((seq_n, 8, chunk), F32),
            pltpu.VMEM((head_n, chunk, hd), BF16),
            pltpu.VMEM((slots, chunk, hd), BF16),
            pltpu.VMEM((halves, seq_n, out_rows, width), BF16),
            pltpu.VMEM((halves, seq_n, out_rows, width), BF16),
            dma((10,)),
            dma((seq_n,)),
            dma((seq_n,)),
            dma((seq_n,)),
            dma((seq_n,)),
            dma((head_n,)),
            dma((head_n,)),
            dma((head_n,)),
            dma((slots,)),
            dma((halves, seq_n)),
            dma((halves, seq_n)),
        ],
        compiler_params=pltpu.CompilerParams(
            collective_id=0, has_side_effects=True, vmem_limit_bytes=64 * 1000 * 1000
        ),
        name="tree_attention",
    )(
        block_ids.reshape(pair_dev, 1, block_ids.shape[1]),
        ancestors,
        jnp.asarray(spread, BF16),
        jnp.asarray(order, BF16),
        tree_keys.reshape(blocks, nodes, hd),
        tree_values.reshape(blocks, nodes, hd),
        queries.reshape(blocks, rows, hd),
        cache_keys,
        cache_values,
        out_weight,
    )
    final = (node_dev, requests, columns)
    mixed = mixed.reshape((2,) + final)
    return mixed[0], mixed[1]


def solution(mesh):
    in_specs = (
        P(None, "head", None, None, None),
        P(None, "head", None, None),
        P(None, "head", None, None),
        P("head", "seq", None),
        P("head", "seq", None),
        P("head", None),
        P(),
        P("seq", "head"),
    )
    out_specs = (P("seq", None, "head"), P("seq", None, "head"))
    return jax.shard_map(local, mesh=mesh, in_specs=in_specs, out_specs=out_specs, check_vma=False)
```

```python
import functools
import math

import jax
import jax.numpy as jnp
import numpy as np
from jax import lax
from jax.experimental import pallas as pl
from jax.experimental.pallas import tpu as pltpu
from jax.sharding import PartitionSpec as P

KVH = 8
BLOCK = 128
MESH = pl.DeviceIdType.MESH
F32 = jnp.float32
BF16 = jnp.bfloat16


def flip(index, mask):
    out = index
    bit = 1
    while bit <= mask:
        if mask & bit:
            out = out + bit * (1 - 2 * ((index // bit) % 2))
        bit *= 2
    return out


def contract(left, right, left_dim, right_dim):
    return lax.dot_general(
        left, right, (((left_dim,), (right_dim,)), ((), ())), preferred_element_type=F32
    )


def kernel(
    dims,
    ids_hbm,
    anc_hbm,
    spread_hbm,
    order_hbm,
    tk_hbm,
    tv_hbm,
    q_hbm,
    k_hbm,
    v_hbm,
    w_hbm,
    out_ref,
    ids_ref,
    anc_ref,
    spread_ref,
    order_ref,
    tk_ref,
    tv_ref,
    q_v,
    k_v,
    v_v,
    w_v,
    acc_out,
    stat_out,
    acc_in,
    stat_in,
    done_rows,
    parts,
    mix_out,
    mix_in,
    load_sem,
    s1,
    r1,
    s1s,
    r1s,
    s2,
    r2,
    s4,
    r4,
):
    seq_n, head_n, pair_dev, groups, nodes, requests, hd, heads_dev = dims
    me = lax.axis_index("seq")
    z = lax.axis_index("head")
    blocks = 2 * pair_dev
    per_block = seq_n // blocks
    rows = groups * nodes
    chunk = rows // per_block
    chunk_heads = chunk // nodes
    pieces = heads_dev // chunk_heads
    ctx = k_v.shape[1]
    blocks_dev = ctx // BLOCK
    node_dev = nodes // seq_n
    out_rows = 2 * node_dev * requests
    factor2 = hd ** (-0.5) * math.log2(math.e)

    loads = []
    sources = (ids_hbm, q_hbm, k_hbm, v_hbm, tk_hbm, tv_hbm, anc_hbm, spread_hbm, order_hbm, w_hbm)
    places = (ids_ref, q_v, k_v, v_v, tk_ref, tv_ref, anc_ref, spread_ref, order_ref, w_v)
    for i, (src, dst) in enumerate(zip(sources, places)):
        copy = pltpu.make_async_copy(src, dst, load_sem.at[i])
        if i < len(places) - 1:
            copy.start()
        loads.append(copy)

    barrier = pltpu.get_barrier_semaphore()
    for k in range(1, seq_n):
        pl.semaphore_signal(barrier, inc=1, device_id={"seq": flip(me, k)}, device_id_type=MESH)
    own_block = me // per_block
    own_piece = me % per_block
    own_attention = own_block // pair_dev
    own_pair = own_block % pair_dev
    own_whole = z * pair_dev + own_pair
    first_head = (own_whole % KVH) * groups + own_piece * chunk_heads
    holder = first_head // heads_dev
    slot = (own_attention * requests + own_whole // KVH) * pieces + (
        first_head % heads_dev
    ) // chunk_heads
    for k in range(1, head_n):
        pl.semaphore_signal(
            barrier,
            inc=1,
            device_id={"seq": holder, "head": flip(z, k)},
            device_id_type=MESH,
        )
    greeted = seq_n + head_n - 2
    own_kv = (me * heads_dev) // groups
    base_piece = (me * heads_dev) % groups // chunk_heads
    for r in range(requests):
        source_pair = r * KVH + own_kv
        plane = source_pair // pair_dev
        other = plane != z
        greeted = greeted + 2 * pieces * other.astype(jnp.int32)
        for a in range(2):
            source = (a * pair_dev + source_pair % pair_dev) * per_block + base_piece
            for piece in range(pieces):

                @pl.when(other)
                def _(source=source + piece, plane=plane):
                    pl.semaphore_signal(
                        barrier,
                        inc=1,
                        device_id={"seq": source, "head": plane},
                        device_id_type=MESH,
                    )

    for copy in loads[:3]:
        copy.wait()
    loads[-1].start()
    owned = me * blocks_dev + lax.broadcasted_iota(jnp.int32, (blocks_dev, 1), 0)

    sends = []
    for step in reversed(range(blocks)):
        block = flip(own_block, step)
        attention = block // pair_dev
        pair = block % pair_dev
        hit = (ids_ref[pair] == owned).astype(F32)
        chosen = jnp.max(hit, axis=1, keepdims=True)
        chosen = jnp.maximum(chosen, attention.astype(F32))
        bias = (chosen - 1.0) * 1e30
        scores = contract(k_v[pair], q_v[block], 1, 1)
        masked = [
            scores[b * BLOCK : (b + 1) * BLOCK] + bias[b : b + 1, :] for b in range(blocks_dev)
        ]
        top = functools.reduce(jnp.maximum, masked)
        peak = jnp.max(top, axis=0, keepdims=True)
        weights = [jnp.exp2((part - peak) * factor2) for part in masked]
        total = jnp.sum(functools.reduce(jnp.add, weights), axis=0, keepdims=True)
        rounded = jnp.concatenate([part.astype(BF16) for part in weights], axis=0)
        if step == blocks - 1:
            loads[3].wait()
        summed = contract(v_v[pair], rounded, 0, 0)
        for piece in range(per_block):
            columns = slice(piece * chunk, (piece + 1) * chunk)
            acc_out[step, piece] = summed[:, columns].astype(BF16)
            stat_out[step, piece, 0:1, :] = peak[:, columns]
            stat_out[step, piece, 1:2, :] = total[:, columns]
        if step == blocks - 1:
            pl.semaphore_wait(barrier, greeted)
        for j in range(per_block):
            k = step * per_block + j
            if k == 0:
                continue
            piece = flip(own_piece, j)
            target = flip(me, k)
            for src, dst, ss, rs in (
                (acc_out, acc_in, s1, r1),
                (stat_out, stat_in, s1s, r1s),
            ):
                copy = pltpu.make_async_remote_copy(
                    src_ref=src.at[step, piece],
                    dst_ref=dst.at[k],
                    send_sem=ss.at[k],
                    recv_sem=rs.at[k],
                    device_id={"seq": target},
                    device_id_type=MESH,
                )
                copy.start()
                sends.append(copy)
    first = list(sends)

    for copy in loads[4:8]:
        copy.wait()
    request = own_whole // KVH
    own_rows = q_v[own_block, pl.ds(pl.multiple_of(own_piece * chunk, chunk), chunk), :]
    tree_scores = contract(tk_ref[own_block], own_rows, 1, 1)
    allowed = contract(anc_ref[request].astype(F32).astype(BF16), spread_ref[...], 0, 0)
    tree_scores = jnp.where(allowed > 0.5, tree_scores, -1e30)
    tree_peak = jnp.max(tree_scores, axis=0, keepdims=True)
    tree_weights = jnp.exp2((tree_scores - tree_peak) * factor2)
    tree_total = jnp.sum(tree_weights, axis=0, keepdims=True)
    tree_sum = contract(tv_ref[own_block], tree_weights.astype(BF16), 0, 0)

    for copy in first:
        copy.wait_recv()
    peaks = [tree_peak, stat_out[0, own_piece, 0:1, :]]
    totals = [tree_total, stat_out[0, own_piece, 1:2, :]]
    for k in range(1, seq_n):
        peaks.append(stat_in[k, 0:1, :])
        totals.append(stat_in[k, 1:2, :])
    highest = functools.reduce(jnp.maximum, peaks)
    factors = [jnp.exp2((peak - highest) * factor2) for peak in peaks]
    total = functools.reduce(jnp.add, [t * f for t, f in zip(totals, factors)])
    summed = tree_sum * factors[0] + acc_out[0, own_piece].astype(F32) * factors[1]
    for k in range(1, seq_n):
        summed = summed + acc_in[k].astype(F32) * factors[k + 1]
    done_rows[...] = jnp.transpose(summed / total).astype(BF16)

    hops = []
    for k in reversed(range(head_n)):
        remote = pltpu.make_async_remote_copy(
            src_ref=done_rows,
            dst_ref=parts.at[slot],
            send_sem=s2.at[k],
            recv_sem=r2.at[slot],
            device_id={"seq": holder, "head": flip(z, k)},
            device_id_type=MESH,
        )
        if k > 0:
            remote.start()
            hops.append(remote)
            continue
        here = pltpu.make_async_copy(done_rows, parts.at[slot], r2.at[slot])

        @pl.when(holder != me)
        def _():
            remote.start()

        @pl.when(holder == me)
        def _():
            here.start()

        near = remote

    for copy in loads[8:]:
        copy.wait()
    for slot in range(2 * requests * pieces):
        pltpu.make_async_copy(done_rows, parts.at[slot], r2.at[slot]).wait()
    stacked = jnp.concatenate(
        [
            jnp.concatenate(
                [
                    parts[lead * pieces + piece, h * nodes : (h + 1) * nodes, :]
                    for piece in range(pieces)
                    for h in range(chunk_heads)
                ],
                axis=1,
            )
            for lead in range(2 * requests)
        ],
        axis=0,
    )
    ordered = contract(order_ref[...], stacked, 1, 0).astype(BF16)
    columns = w_v.shape[1]
    halves = mix_out.shape[0]
    width = columns // halves
    last = []
    for half in range(halves):
        mixed = contract(ordered, w_v[:, half * width : (half + 1) * width], 1, 0)
        for t in range(seq_n):
            mix_out[half, t] = mixed[t * out_rows : (t + 1) * out_rows].astype(BF16)
        for k in reversed(range(1, seq_n)):
            target = flip(me, k)
            copy = pltpu.make_async_remote_copy(
                src_ref=mix_out.at[half, target],
                dst_ref=mix_in.at[half, k],
                send_sem=s4.at[half, k],
                recv_sem=r4.at[half, k],
                device_id={"seq": target},
                device_id_type=MESH,
            )
            copy.start()
            last.append((half, copy))
    for half in range(halves):
        for h, copy in last:
            if h == half:
                copy.wait_recv()
        result = mix_out[half, me].astype(F32)
        for k in range(1, seq_n):
            result = result + mix_in[half, k].astype(F32)
        span = slice(half * width, (half + 1) * width)
        out_ref[:, span] = result.astype(BF16)

    for copy in first:
        copy.wait_send()
    for copy in hops:
        copy.wait_send()

    @pl.when(holder != me)
    def _():
        near.wait_send()

    for _, copy in last:
        copy.wait_send()


def local(
    queries, tree_keys, tree_values, cache_keys, cache_values, block_ids, ancestors, out_weight
):
    _, pair_dev, groups, nodes, hd = queries.shape
    ctx = cache_keys.shape[1]
    requests = ancestors.shape[0]
    rows_dev, columns = out_weight.shape
    seq_n = lax.axis_size("seq")
    head_n = lax.axis_size("head")
    heads_dev = rows_dev // hd
    blocks = 2 * pair_dev
    per_block = seq_n // blocks
    rows = groups * nodes
    chunk = rows // per_block
    node_dev = nodes // seq_n
    halves = 1
    width = columns // halves
    out_rows = 2 * node_dev * requests
    all_rows = 2 * requests * nodes
    slots = 2 * requests * heads_dev * nodes // chunk

    spread = (np.arange(chunk)[None, :] % nodes == np.arange(nodes)[:, None]).astype(np.float32)
    order = np.zeros((all_rows, all_rows), np.float32)
    for a in range(2):
        for r in range(requests):
            for n in range(nodes):
                t, j = divmod(n, node_dev)
                row = t * out_rows + a * (node_dev * requests) + j * requests + r
                order[row, (a * requests + r) * nodes + n] = 1.0

    dims = (seq_n, head_n, pair_dev, groups, nodes, requests, hd, heads_dev)
    vmem = pl.BlockSpec(memory_space=pltpu.VMEM)
    hbm = pl.BlockSpec(memory_space=pltpu.HBM)
    shape = jax.ShapeDtypeStruct((out_rows, columns), BF16)
    dma = pltpu.SemaphoreType.DMA
    mixed = pl.pallas_call(
        functools.partial(kernel, dims),
        out_shape=shape,
        in_specs=[hbm] * 10,
        out_specs=vmem,
        scratch_shapes=[
            pltpu.VMEM((pair_dev, 1, block_ids.shape[1]), jnp.int32),
            pltpu.VMEM((requests, nodes, nodes), jnp.int32),
            pltpu.VMEM(spread.shape, BF16),
            pltpu.VMEM(order.shape, BF16),
            pltpu.VMEM((blocks, nodes, hd), BF16),
            pltpu.VMEM((blocks, nodes, hd), BF16),
            pltpu.VMEM((blocks, rows, hd), BF16),
            pltpu.VMEM((pair_dev, ctx, hd), BF16),
            pltpu.VMEM((pair_dev, ctx, hd), BF16),
            pltpu.VMEM((rows_dev, columns), BF16),
            pltpu.VMEM((blocks, per_block, hd, chunk), BF16),
            pltpu.VMEM((blocks, per_block, 8, chunk), F32),
            pltpu.VMEM((seq_n, hd, chunk), BF16),
            pltpu.VMEM((seq_n, 8, chunk), F32),
            pltpu.VMEM((chunk, hd), BF16),
            pltpu.VMEM((slots, chunk, hd), BF16),
            pltpu.VMEM((halves, seq_n, out_rows, width), BF16),
            pltpu.VMEM((halves, seq_n, out_rows, width), BF16),
            dma((10,)),
            dma((seq_n,)),
            dma((seq_n,)),
            dma((seq_n,)),
            dma((seq_n,)),
            dma((head_n,)),
            dma((slots,)),
            dma((halves, seq_n)),
            dma((halves, seq_n)),
        ],
        compiler_params=pltpu.CompilerParams(
            collective_id=0, has_side_effects=True, vmem_limit_bytes=64 * 1000 * 1000
        ),
        name="tree_attention",
    )(
        block_ids.reshape(pair_dev, 1, block_ids.shape[1]),
        ancestors,
        jnp.asarray(spread, BF16),
        jnp.asarray(order, BF16),
        tree_keys.reshape(blocks, nodes, hd),
        tree_values.reshape(blocks, nodes, hd),
        queries.reshape(blocks, rows, hd),
        cache_keys,
        cache_values,
        out_weight,
    )
    final = (node_dev, requests, columns)
    mixed = mixed.reshape((2,) + final)
    return mixed[0], mixed[1]


def solution(mesh):
    in_specs = (
        P(None, "head", None, None, None),
        P(None, "head", None, None),
        P(None, "head", None, None),
        P("head", "seq", None),
        P("head", "seq", None),
        P("head", None),
        P(),
        P("seq", "head"),
    )
    out_specs = (P("seq", None, "head"), P("seq", None, "head"))
    return jax.shard_map(local, mesh=mesh, in_specs=in_specs, out_specs=out_specs, check_vma=False)
```
